256 devices in a mesh: blk: 32 (over z, x_hi, core), col: 8 (over y, x_lo).
Axes of the slice: x: 4 (x_hi: 2, x_lo: 2; x = x_hi * 2 + x_lo), y: 4, z: 8, core: 2. Of those that a mesh axis runs over, the one named last changes fastest.
Arguments:
- targets: bfloat16 [32, 48, 72, 96], P('blk'), may hold values from -6 to 6
- sources: bfloat16 [512, 48, 72, 96], P(('blk', 'col')), may hold values from -6 to 6
- band_of_slot: int32 [512], P(('blk', 'col')), may hold values from 0 to 511, each once
- occupied: int32 [512], replicated, may hold values 0 or 1
Outputs:
- fock: float32 [32, 48, 72, 96], P('blk', 'col')
The draws below stay inside these ranges and needn't reach their ends.
Inputs may be any that keep to these rules, and one draw needn't show every extreme that they name: `band_of_slot`: every band number appears in exactly one slot.
All inputs are finite; a program needn't handle non-finite values.
Results may differ from the reference program's by a relative error of at most 0.0003.
Values may be sent and summed in bfloat16 or wider, within the bound.
No kernel may reach another device: no remote copies, remote signals or barrier semaphores. Data moves between devices by JAX's collectives and lax.ppermute only.
A program may use at most 64 MiB of HBM per device.

```python
import math
import jax
import jax.numpy as jnp
from jax import lax

NX = 48
NY = 72
NZ = 96
TARG_DEV = 1
SRC_DEV = 2
HOPS = 2
BANDS = 32
SOURCES = 512
N_BLK = 32
N_COL = 8


def plant(values, key, smallest, high):
    place = [jax.random.randint(jax.random.fold_in(key, axis), (), 0, length) for axis, length in enumerate(values.shape)]
    longest = values.shape.index(max(values.shape))
    next_to = place[:longest] + [(place[longest] + 1) % values.shape[longest]] + place[longest + 1:]
    return values.at[tuple(place)].set(smallest).at[tuple(next_to)].set(high)


def steps_of(rng, dims, cuts, low, high):
    def one(axis_at, shards_of):
        steps = jax.random.uniform(jax.random.fold_in(jax.random.fold_in(rng, 6), axis_at), (shards_of,), jnp.float32, low / len(cuts), high / len(cuts))
        return jnp.repeat(jnp.exp(steps), dims[axis_at] // shards_of).reshape((-1,) + (1,) * (len(dims) - axis_at - 1))

    factor_of = one(*cuts[0])
    for cut in cuts[1:]:
        factor_of = factor_of * one(*cut)
    return factor_of


def centred(own_key, shape, deviation, most, cuts=(), held_as=jnp.bfloat16):
    values = deviation * jax.random.normal(own_key, shape, jnp.float32)
    if cuts:
        values = values * steps_of(own_key, shape, cuts, -0.22, 0.18)
    return jnp.clip(values, -most, most).astype(held_as)


def setup_inputs(seed: int = 0) -> dict:
    key_list = jax.random.split(jax.random.key(seed), 5)
    return {
        "targets": centred(key_list[0], (BANDS, NX, NY, NZ), 1.0, 6.0, ((0, 32),)),
        "sources": centred(key_list[1], (SOURCES, NX, NY, NZ), 1.0, 6.0, ((0, 256),)),
        "band_of_slot": jax.random.permutation(key_list[2], SOURCES).astype(jnp.int32),
        "occupied": plant((jax.random.randint(key_list[3], (SOURCES,), 0, 4) < 3).astype(jnp.int32), jax.random.fold_in(key_list[3], 1), 0, 1),
    }


grid_spacing = 0.3
screening = 0.11


def frequency_sq(length):
    index_row = jnp.arange(length, dtype=jnp.int32)
    periodic = jnp.minimum(index_row, length - index_row).astype(jnp.float32)
    return (2.0 * math.pi * periodic / (length * grid_spacing)) ** 2


def kernel_field(size_x, size_y, size_z):
    g_sq = frequency_sq(size_x)[:, None, None] + frequency_sq(size_y)[None, :, None] + frequency_sq(size_z)[None, None, :]
    safe_sq = jnp.where(g_sq > 0, g_sq, jnp.float32(1.0))
    value = 4.0 * math.pi / safe_sq * (1.0 - jnp.exp(-safe_sq / (4.0 * screening * screening)))
    return jnp.where(g_sq > 0, value, jnp.float32(math.pi / (screening * screening))).astype(jnp.float32)


def reference(targets, sources, band_of_slot, occupied):
    weights = jnp.where(occupied[band_of_slot] > 0, 1.0, 0.0).astype(jnp.float32)
    per_block = N_COL * SRC_DEV
    src_blocks = sources.astype(jnp.float32).reshape(N_BLK, per_block, NX, NY, NZ)
    weight_blocks = weights.reshape(N_BLK, per_block)
    coulomb = kernel_field(NX, NY, NZ)[:, :, : NZ // 2 + 1]

    def one_target(band_index):
        psi = targets[band_index].astype(jnp.float32)
        block_index = band_index // TARG_DEV
        accum = jnp.zeros((NX, NY, NZ), jnp.float32)
        for hop_index in range(HOPS + 1):
            src_index = (block_index - hop_index) % N_BLK
            orbitals = src_blocks[src_index]
            occup = weight_blocks[src_index]
            pair_field = psi[None] * orbitals
            spectrum = jnp.fft.rfftn(pair_field, axes=(1, 2, 3))
            potential = jnp.fft.irfftn(spectrum * coulomb, s=(NX, NY, NZ), axes=(1, 2, 3))
            accum = accum + jnp.sum(potential * orbitals * occup[:, None, None, None], axis=0)
        return -0.125 * accum

    return lax.map(one_target, jnp.arange(BANDS, dtype=jnp.int32))
```

```python
import math

import jax
import jax.numpy as jnp
import ml_dtypes
import numpy as np
from jax import lax
from jax.experimental import pallas as pl
from jax.experimental.pallas import tpu as pltpu
from jax.sharding import PartitionSpec as P

NX, NY, NZ = 48, 72, 96
LANES = 128
BASE = 36
TAIL = NX - BASE
N_BLK, N_COL = 32, 8
SLICE = NX // N_COL
TILES = SLICE * NY // 8
KEPT = 41
SPARE = TILES - KEPT
AXES = ("blk", "col")
F32, BF16 = jnp.float32, jnp.bfloat16
grid_spacing = 0.3
screening = 0.11


def basis_of(length):
    row, col = np.arange(length)[:, None], np.arange(length)[None, :]
    angle = 2.0 * np.pi / length * (row * col % length)
    table = np.where(row <= length // 2, np.cos(angle), np.sin(angle))
    edge = (row == 0) | (row == length // 2)
    return table * np.where(edge, math.sqrt(1.0 / length), math.sqrt(2.0 / length))


def halves(table):
    high = table.astype(ml_dtypes.bfloat16)
    return high, (table - high.astype(np.float64)).astype(ml_dtypes.bfloat16)


def left_operand(table, pad):
    high, low = halves(table)
    gap = np.zeros((table.shape[0], pad), ml_dtypes.bfloat16)
    return np.concatenate([high, gap, high, gap, low, gap], axis=1)


def right_operand(table):
    size = table.shape[0]
    high, low = halves(table)
    out = np.zeros((2 * LANES, 2 * LANES), ml_dtypes.bfloat16)
    for row in (0, LANES):
        out[row : row + size, :size] = high
        out[row : row + size, LANES : LANES + size] = low
    return out


def frequency_sq(length):
    index = np.arange(length)
    return (2.0 * np.pi * np.minimum(index, length - index) / (length * grid_spacing)) ** 2


def kernel_field():
    g_sq = (
        frequency_sq(NY)[:, None, None] + frequency_sq(NX)[None, :, None] + frequency_sq(NZ)[None, None, :]
    )
    safe_sq = np.where(g_sq > 0, g_sq, 1.0)
    value = 4.0 * np.pi / safe_sq * (1.0 - np.exp(-safe_sq / (4.0 * screening * screening)))
    value = -0.125 * np.where(g_sq > 0, value, np.pi / (screening * screening))
    out = np.zeros((NY, NX, LANES), np.float32)
    out[:, :, :NZ] = value
    return out.reshape(NY * NX, LANES)


def constants():
    basis_x, basis_y, basis_z = basis_of(NX), basis_of(NY), basis_of(NZ)
    tables = (
        kernel_field(),
        left_operand(basis_y, 8),
        left_operand(basis_x, 0),
        right_operand(basis_z.T),
        right_operand(basis_z),
        left_operand(basis_x.T, 0),
        left_operand(basis_y.T, 8),
    )
    return tuple(jnp.asarray(table) for table in tables)


def dot(left, right):
    return jnp.dot(left, right, preferred_element_type=F32)


def split(value):
    high = value.astype(BF16)
    return high, (value - high.astype(F32)).astype(BF16)


def stacked(value):
    high, low = split(value)
    return jnp.concatenate([high, low, high], axis=0)


def stacked_y(value):
    return stacked(jnp.concatenate([value, jnp.zeros((8, LANES), F32)], axis=0))


def side(value):
    high, low = split(value)
    return jnp.concatenate([high, low], axis=1)


def folded(value):
    return value[:, :LANES] + value[:, LANES:]


def columns(value, which):
    return value[:, LANES * which : LANES * (which + 1)]


def lane_of(rows):
    return lax.broadcasted_iota(jnp.int32, (rows, LANES), 1)


def pack_kernel(band_ref, occupied_ref, source_ref, out_ref, *, slot):
    weight = jnp.where(occupied_ref[band_ref[slot]] > 0, 1.0, 0.0).astype(F32)
    for third in range(3):

        def step(index, carry):
            plane = third * TAIL + index
            base = source_ref[0, plane].astype(F32)
            tail = source_ref[0, BASE + index][:, 32 * third : 32 * third + 32].astype(F32)
            row = jnp.concatenate([base, tail], axis=1) * weight
            out_ref[plane] = row.astype(BF16)
            return carry

        lax.fori_loop(0, TAIL, step, 0, unroll=4)


def packed(sources, slot, band_of_slot, occupied):
    return pl.pallas_call(
        lambda *refs: pack_kernel(*refs, slot=slot),
        out_shape=jax.ShapeDtypeStruct((BASE, NY, LANES), BF16),
        grid=(1,),
        in_specs=[
            pl.BlockSpec(memory_space=pltpu.SMEM),
            pl.BlockSpec(memory_space=pltpu.SMEM),
            pl.BlockSpec((1, NX, NY, NZ), lambda i: (slot, 0, 0, 0)),
        ],
        out_specs=pl.BlockSpec((BASE, NY, LANES), lambda i: (0, 0, 0)),
        name="pack",
    )(band_of_slot, occupied, sources)


def unpack_tail(source_refs, tail_ref):
    lane = lane_of(NY)

    def step(index, carry):
        parts = []
        for third in range(3):
            part = sum(ref[index + third * TAIL].astype(F32) for ref in source_refs)
            parts.append(pltpu.roll(part, 32 * third + 32, 1))
        plane = jnp.where(lane < 32, parts[0], jnp.where(lane < 64, parts[1], parts[2]))
        tail_ref[index] = plane.astype(BF16)
        return carry

    lax.fori_loop(0, TAIL, step, 0, unroll=4)


def solve_kernel(*refs, n_sources, has_accum, last):
    target_ref = refs[0]
    source_refs = refs[1 : 1 + n_sources]
    coulomb, left_y, left_x, right_z, right_k, left_p, left_q = refs[1 + n_sources : 8 + n_sources]
    rest = refs[8 + n_sources :]
    if has_accum:
        accum_in, rest = rest[0], rest[1:]
    out_ref, by_x, by_y, tail_ref, *more = rest
    accum = more[0] if last else out_ref

    unpack_tail(source_refs, tail_ref)

    def plane_of(plane):
        if plane >= BASE:
            return tail_ref[plane - BASE].astype(F32)
        return sum(ref[plane].astype(F32) for ref in source_refs)

    for plane in range(0, NX, 2):
        pair = [target_ref[p].astype(F32) * plane_of(p) for p in (plane, plane + 1)]
        spectrum = dot(left_y[...], jnp.concatenate([stacked_y(p) for p in pair], axis=1))
        for which in range(2):
            by_x[pl.ds(plane + which, NY, stride=NX), :] = columns(spectrum, which)

    group = 36

    def middle(step, carry):
        first = step * group
        rows = []
        for row in range(0, group, 2):
            lines = [
                by_x[pl.ds(pl.multiple_of((first + row + which) * NX, 8), NX), :] for which in range(2)
            ]
            spectrum = dot(left_x[...], jnp.concatenate([stacked(line) for line in lines], axis=1))
            rows += [side(columns(spectrum, which)) for which in range(2)]
        spectrum = folded(dot(jnp.concatenate(rows, axis=0), right_z[...]))
        spectrum = spectrum * coulomb[pl.ds(pl.multiple_of(first * NX, 8), group * NX), :]
        field = folded(dot(side(spectrum), right_k[...]))
        for row in range(0, group, 2):
            lines = [field[(row + which) * NX : (row + which + 1) * NX] for which in range(2)]
            part = dot(left_p[...], jnp.concatenate([stacked(line) for line in lines], axis=1))
            for which in range(2):
                by_y[pl.ds(first + row + which, NX, stride=NY), :] = columns(part, which)
        return carry

    lax.fori_loop(0, NY // group, middle, 0)

    for plane in range(0, NX, 2):
        lines = [by_y[(plane + which) * NY : (plane + which + 1) * NY, :] for which in range(2)]
        potential = dot(left_q[...], jnp.concatenate([stacked_y(line) for line in lines], axis=1))
        for which in range(2):
            term = columns(potential, which) * plane_of(plane + which)
            if has_accum:
                term = term + accum_in[plane + which]
            accum[plane + which] = term

    if last:
        lane = lane_of(8)

        def tile_of(piece, tile):
            plane, row = divmod(tile, NY // 8)
            return accum[piece * SLICE + plane, 8 * row : 8 * row + 8, :]

        def pack_slice(piece, carry):
            for tile in range(KEPT):
                value = tile_of(piece, tile)
                third, index = divmod(tile, SPARE)
                if third < 3:
                    spare = pltpu.roll(tile_of(piece, KEPT + index), 96 - 32 * third, 1)
                    value = jnp.where(lane < 96, value, spare)
                out_ref[piece, 8 * tile : 8 * tile + 8, :] = value
            return carry

        lax.fori_loop(0, N_COL, pack_slice, 0)


def solved(target, source_list, tables, accum=None, last=False):
    whole = pl.BlockSpec(memory_space=pltpu.VMEM)
    operands = [target, *source_list, *tables] + ([accum] if accum is not None else [])
    scratch = [
        pltpu.VMEM((NX * NY, LANES), F32),
        pltpu.VMEM((NX * NY, LANES), F32),
        pltpu.VMEM((TAIL, NY, LANES), BF16),
    ]
    if last:
        shape = (N_COL, 8 * KEPT, LANES)
        scratch.append(pltpu.VMEM((NX, NY, LANES), F32))
    else:
        shape = (NX, NY, LANES)
    return pl.pallas_call(
        lambda *refs: solve_kernel(
            *refs, n_sources=len(source_list), has_accum=accum is not None, last=last
        ),
        out_shape=jax.ShapeDtypeStruct(shape, F32),
        in_specs=[whole] * len(operands),
        out_specs=whole,
        scratch_shapes=scratch,
        compiler_params=pltpu.CompilerParams(vmem_limit_bytes=40 << 20),
        cost_estimate=pl.CostEstimate(flops=2_000_000_000, bytes_accessed=4_000_000, transcendentals=0),
        name="solve",
    )(*operands)


def gather_kernel(parts_ref, out_ref, total_ref):
    lane = lane_of(8)
    for tile in range(KEPT):
        rows = slice(8 * tile, 8 * tile + 8)
        total = parts_ref[0, rows, :].astype(F32)
        for part in range(1, N_COL):
            total = total + parts_ref[part, rows, :].astype(F32)
        total_ref[rows, :] = total

    def put(tile, value):
        plane, row = divmod(tile, NY // 8)
        out_ref[0, plane, 8 * row : 8 * row + 8, :] = value[:, :NZ]

    for tile in range(KEPT):
        put(tile, total_ref[8 * tile : 8 * tile + 8, :])
    for index in range(SPARE):
        parts = []
        for third in range(3):
            tile = index + third * SPARE
            parts.append(pltpu.roll(total_ref[8 * tile : 8 * tile + 8, :], 32 * third + 32, 1))
        put(KEPT + index, jnp.where(lane < 32, parts[0], jnp.where(lane < 64, parts[1], parts[2])))


def gathered(parts):
    whole = pl.BlockSpec(memory_space=pltpu.VMEM)
    return pl.pallas_call(
        gather_kernel,
        out_shape=jax.ShapeDtypeStruct((1, SLICE, NY, NZ), F32),
        in_specs=[whole],
        out_specs=whole,
        scratch_shapes=[pltpu.VMEM((8 * KEPT, LANES), F32)],
        name="gather",
    )(parts)


def flat(block, col):
    return block % N_BLK * N_COL + col


def next_block():
    pairs = []
    for block in range(N_BLK):
        for col in range(N_COL):
            pairs.append((flat(block, col), flat(block + 1, col ^ (block % 2))))
    return pairs


def even_ahead():
    return [(flat(b, c), flat(b + 2, c ^ 1)) for b in range(0, N_BLK, 2) for c in range(N_COL)]


def even_to_odd():
    return [(flat(b, c), flat(b + 1, c)) for b in range(0, N_BLK, 2) for c in range(N_COL)]


def shards(targets, sources, band_of_slot, occupied):
    tables = constants()
    own = [packed(sources, slot, band_of_slot, occupied) for slot in range(2)]
    near = [lax.ppermute(value, AXES, next_block()) for value in own]
    far = [lax.ppermute(value, AXES, even_ahead()) for value in own]
    passed = [lax.ppermute(value, AXES, even_to_odd()) for value in near]
    target = jnp.pad(targets[0], ((0, 0), (0, 0), (0, LANES - NZ)))
    accum = solved(target, [own[0]], tables)
    accum = solved(target, [own[1]], tables, accum)
    accum = solved(target, [near[0]], tables, accum)
    accum = solved(target, [near[1]], tables, accum)
    accum = solved(target, [far[0], passed[0]], tables, accum)
    pieces = solved(target, [far[1], passed[1]], tables, accum, last=True)
    parts = lax.all_to_all(pieces, "col", 0, 0)
    return gathered(parts)


def solution(mesh):
    return jax.shard_map(
        shards,
        mesh=mesh,
        in_specs=(
            P("blk", None, None, None),
            P(("blk", "col"), None, None, None),
            P(("blk", "col")),
            P(),
        ),
        out_specs=P("blk", "col", None, None),
        check_vma=False,
    )
```

```python
import math

import jax
import jax.numpy as jnp
import ml_dtypes
import numpy as np
from jax import lax
from jax.experimental import pallas as pl
from jax.experimental.pallas import tpu as pltpu
from jax.sharding import PartitionSpec as P

NX, NY, NZ = 48, 72, 96
LANES = 128
BASE = 36
TAIL = NX - BASE
HALF_Y = NY // 2 + 1
N_BLK, N_COL = 32, 8
SLICE = NX // N_COL
TILES = SLICE * NY // 8
KEPT = 41
SPARE = TILES - KEPT
AXES = ("blk", "col")
F32, BF16 = jnp.float32, jnp.bfloat16
grid_spacing = 0.3
screening = 0.11


def basis_of(length):
    row, col = np.arange(length)[:, None], np.arange(length)[None, :]
    angle = 2.0 * np.pi / length * (row * col % length)
    table = np.where(row <= length // 2, np.cos(angle), np.sin(angle))
    edge = (row == 0) | (row == length // 2)
    return table * np.where(edge, math.sqrt(1.0 / length), math.sqrt(2.0 / length))


def halves(table):
    high = table.astype(ml_dtypes.bfloat16)
    return high, (table - high.astype(np.float64)).astype(ml_dtypes.bfloat16)


def left_operand(table, pad):
    high, low = halves(table)
    gap = np.zeros((table.shape[0], pad), ml_dtypes.bfloat16)
    return np.concatenate([high, gap, high, gap, low, gap], axis=1)


def right_operand(table):
    size = table.shape[0]
    high, low = halves(table)
    out = np.zeros((2 * LANES, 2 * LANES), ml_dtypes.bfloat16)
    for row in (0, LANES):
        out[row : row + size, :size] = high
        out[row : row + size, LANES : LANES + size] = low
    return out


def frequency_sq(length):
    index = np.arange(length)
    return (2.0 * np.pi * np.minimum(index, length - index) / (length * grid_spacing)) ** 2


def kernel_field():
    g_sq = (
        frequency_sq(NY)[: HALF_Y, None, None]
        + frequency_sq(NX)[None, :, None]
        + frequency_sq(NZ)[None, None, :]
    )
    safe_sq = np.where(g_sq > 0, g_sq, 1.0)
    value = 4.0 * np.pi / safe_sq * (1.0 - np.exp(-safe_sq / (4.0 * screening * screening)))
    value = -0.125 * np.where(g_sq > 0, value, np.pi / (screening * screening))
    out = np.zeros((HALF_Y, NX, LANES), np.float32)
    out[:, :, :NZ] = value
    return out.reshape(HALF_Y * NX, LANES)


def constants():
    basis_x, basis_y, basis_z = basis_of(NX), basis_of(NY), basis_of(NZ)
    tables = (
        kernel_field(),
        left_operand(basis_y, 8),
        left_operand(basis_x, 0),
        right_operand(basis_z.T),
        right_operand(basis_z),
        left_operand(basis_x.T, 0),
        left_operand(basis_y.T, 8),
    )
    return tuple(jnp.asarray(table) for table in tables)


def dot(left, right):
    return jnp.dot(left, right, preferred_element_type=F32)


def split(value):
    high = value.astype(BF16)
    return high, (value - high.astype(F32)).astype(BF16)


def stacked(value):
    high, low = split(value)
    return jnp.concatenate([high, low, high], axis=0)


def stacked_y(value):
    return stacked(jnp.concatenate([value, jnp.zeros((8, LANES), F32)], axis=0))


def side(value):
    high, low = split(value)
    return jnp.concatenate([high, low], axis=1)


def folded(value):
    return value[:, :LANES] + value[:, LANES:]


def columns(value, which):
    return value[:, LANES * which : LANES * (which + 1)]


def widened(value):
    gap = jnp.zeros((value.shape[0], LANES - NZ), F32)
    return jnp.concatenate([value.astype(F32), gap], axis=1)


def lane_of(rows):
    return lax.broadcasted_iota(jnp.int32, (rows, LANES), 1)


def pack_kernel(band_ref, occupied_ref, source_ref, first_ref, second_ref, held, full, in_sems, out_sems):
    chunks = NX // TAIL
    planes = [pl.ds(chunk * TAIL, TAIL) for chunk in range(chunks)]
    order = [(slot, chunk) for slot in range(2) for chunk in (chunks - 1, *range(chunks - 1))]
    reads = {}
    for slot, chunk in order:
        reads[slot, chunk] = pltpu.make_async_copy(
            source_ref.at[slot, planes[chunk]], held.at[slot, planes[chunk]], in_sems.at[slot, chunk]
        )
        reads[slot, chunk].start()
    lane = lane_of(NY)
    writes = []
    for slot, out_ref in enumerate((first_ref, second_ref)):
        weight = jnp.where(occupied_ref[band_ref[slot]] > 0, 1.0, 0.0).astype(F32)
        reads[slot, chunks - 1].wait()
        for third in range(chunks - 1):
            reads[slot, third].wait()
            for index in range(TAIL):
                plane = third * TAIL + index
                base = widened(held[slot, plane])
                tail = pltpu.roll(widened(held[slot, BASE + index]), 96 - 32 * third, 1)
                full[slot, plane] = (jnp.where(lane < 96, base, tail) * weight).astype(BF16)
            write = pltpu.make_async_copy(
                full.at[slot, planes[third]], out_ref.at[planes[third]], out_sems.at[slot, third]
            )
            write.start()
            writes.append(write)
    for write in writes:
        write.wait()


def packed(sources, band_of_slot, occupied):
    anywhere = pl.BlockSpec(memory_space=pl.ANY)
    scalars = pl.BlockSpec(memory_space=pltpu.SMEM)
    shape = jax.ShapeDtypeStruct((BASE, NY, LANES), BF16)
    return pl.pallas_call(
        pack_kernel,
        out_shape=(shape, shape),
        in_specs=[scalars, scalars, anywhere],
        out_specs=(anywhere, anywhere),
        scratch_shapes=[
            pltpu.VMEM((2, NX, NY, NZ), BF16),
            pltpu.VMEM((2, BASE, NY, LANES), BF16),
            pltpu.SemaphoreType.DMA((2, NX // TAIL)),
            pltpu.SemaphoreType.DMA((2, BASE // TAIL)),
        ],
        compiler_params=pltpu.CompilerParams(vmem_limit_bytes=60 << 20),
        name="pack",
    )(band_of_slot, occupied, sources)


def solve_kernel(*refs, n_sources, has_accum, last):
    target_ref = refs[0]
    source_refs = refs[1 : 1 + n_sources]
    coulomb, left_y, left_x, right_z, right_k, left_p, left_q = refs[1 + n_sources : 8 + n_sources]
    rest = refs[8 + n_sources :]
    if has_accum:
        accum_in, rest = rest[0], rest[1:]
    out_ref, by_x, by_y, tail_ref, *more = rest
    accum = more[0] if last else out_ref

    lane = lane_of(NY)

    def held_plane(plane):
        return sum(ref[plane].astype(F32) for ref in source_refs)

    def first_plane(plane):
        if plane < BASE:
            return held_plane(plane)
        parts = [
            pltpu.roll(held_plane(plane - BASE + third * TAIL), 32 * third + 32, 1) for third in range(3)
        ]
        value = jnp.where(lane < 32, parts[0], jnp.where(lane < 64, parts[1], parts[2]))
        tail_ref[plane - BASE] = value.astype(BF16)
        return value

    def plane_of(plane):
        return held_plane(plane) if plane < BASE else tail_ref[plane - BASE].astype(F32)

    for plane in range(0, NX, 2):
        pair = [widened(target_ref[0, p]) * first_plane(p) for p in (plane, plane + 1)]
        spectrum = dot(left_y[...], jnp.concatenate([stacked_y(p) for p in pair], axis=1))
        for which in range(2):
            by_x[pl.ds(plane + which, NY, stride=NX), :] = columns(spectrum, which)

    group = 36

    def middle(step, carry):
        first = step * group
        rows = []
        for row in range(0, group, 2):
            lines = [
                by_x[pl.ds(pl.multiple_of((first + row + which) * NX, 8), NX), :] for which in range(2)
            ]
            spectrum = dot(left_x[...], jnp.concatenate([stacked(line) for line in lines], axis=1))
            rows += [side(columns(spectrum, which)) for which in range(2)]
        spectrum = folded(dot(jnp.concatenate(rows, axis=0), right_z[...]))
        field = []
        for row in range(group):
            freq = jnp.minimum(first + row, NY - first - row)
            field.append(coulomb[pl.ds(pl.multiple_of(freq * NX, 8), NX), :])
        spectrum = spectrum * jnp.concatenate(field, axis=0)
        field = folded(dot(side(spectrum), right_k[...]))
        for row in range(0, group, 2):
            lines = [field[(row + which) * NX : (row + which + 1) * NX] for which in range(2)]
            part = dot(left_p[...], jnp.concatenate([stacked(line) for line in lines], axis=1))
            for which in range(2):
                by_y[pl.ds(first + row + which, NX, stride=NY), :] = columns(part, which)
        return carry

    lax.fori_loop(0, NY // group, middle, 0)

    for plane in range(0, NX, 2):
        lines = [by_y[(plane + which) * NY : (plane + which + 1) * NY, :] for which in range(2)]
        potential = dot(left_q[...], jnp.concatenate([stacked_y(line) for line in lines], axis=1))
        for which in range(2):
            term = columns(potential, which) * plane_of(plane + which)
            if has_accum:
                term = term + accum_in[plane + which]
            accum[plane + which] = term

    if last:
        tile_lane = lane_of(8)

        def tile_of(piece, tile):
            plane, row = divmod(tile, NY // 8)
            return accum[piece * SLICE + plane, 8 * row : 8 * row + 8, :]

        def pack_slice(piece, carry):
            for tile in range(KEPT):
                value = tile_of(piece, tile)
                third, index = divmod(tile, SPARE)
                if third < 3:
                    spare = pltpu.roll(tile_of(piece, KEPT + index), 96 - 32 * third, 1)
                    value = jnp.where(tile_lane < 96, value, spare)
                out_ref[piece, 8 * tile : 8 * tile + 8, :] = value
            return carry

        lax.fori_loop(0, N_COL, pack_slice, 0)


def solved(target, source_list, tables, accum=None, last=False):
    whole = pl.BlockSpec(memory_space=pltpu.VMEM)
    operands = [target, *source_list, *tables] + ([accum] if accum is not None else [])
    scratch = [
        pltpu.VMEM((NX * NY, LANES), F32),
        pltpu.VMEM((NX * NY, LANES), F32),
        pltpu.VMEM((TAIL, NY, LANES), BF16),
    ]
    if last:
        shape = (N_COL, 8 * KEPT, LANES)
        scratch.append(pltpu.VMEM((NX, NY, LANES), F32))
    else:
        shape = (NX, NY, LANES)
    return pl.pallas_call(
        lambda *refs: solve_kernel(
            *refs, n_sources=len(source_list), has_accum=accum is not None, last=last
        ),
        out_shape=jax.ShapeDtypeStruct(shape, F32),
        in_specs=[whole] * len(operands),
        out_specs=whole,
        scratch_shapes=scratch,
        compiler_params=pltpu.CompilerParams(vmem_limit_bytes=40 << 20),
        cost_estimate=pl.CostEstimate(flops=2_000_000_000, bytes_accessed=4_000_000, transcendentals=0),
        name="solve",
    )(*operands)


def gather_kernel(parts_ref, out_ref, total_ref):
    lane = lane_of(8)
    for tile in range(KEPT):
        rows = slice(8 * tile, 8 * tile + 8)
        total = parts_ref[0, rows, :].astype(F32)
        for part in range(1, N_COL):
            total = total + parts_ref[part, rows, :].astype(F32)
        total_ref[rows, :] = total

    def put(tile, value):
        plane, row = divmod(tile, NY // 8)
        out_ref[0, plane, 8 * row : 8 * row + 8, :] = value[:, :NZ]

    for tile in range(KEPT):
        put(tile, total_ref[8 * tile : 8 * tile + 8, :])
    for index in range(SPARE):
        parts = []
        for third in range(3):
            tile = index + third * SPARE
            parts.append(pltpu.roll(total_ref[8 * tile : 8 * tile + 8, :], 32 * third + 32, 1))
        put(KEPT + index, jnp.where(lane < 32, parts[0], jnp.where(lane < 64, parts[1], parts[2])))


def gathered(parts):
    whole = pl.BlockSpec(memory_space=pltpu.VMEM)
    return pl.pallas_call(
        gather_kernel,
        out_shape=jax.ShapeDtypeStruct((1, SLICE, NY, NZ), F32),
        in_specs=[whole],
        out_specs=whole,
        scratch_shapes=[pltpu.VMEM((8 * KEPT, LANES), F32)],
        name="gather",
    )(parts)


def flat(block, col):
    return block % N_BLK * N_COL + col


def next_block():
    pairs = []
    for block in range(N_BLK):
        for col in range(N_COL):
            pairs.append((flat(block, col), flat(block + 1, col ^ (block % 2))))
    return pairs


def even_ahead():
    return [(flat(b, c), flat(b + 2, c ^ 1)) for b in range(0, N_BLK, 2) for c in range(N_COL)]


def even_to_odd():
    return [(flat(b, c), flat(b + 1, c)) for b in range(0, N_BLK, 2) for c in range(N_COL)]


def sent(value, pairs):
    return lax.ppermute(value, AXES, pairs)


def shards(targets, sources, band_of_slot, occupied):
    tables = constants()
    own = packed(sources, band_of_slot, occupied)
    near = [sent(own[slot], next_block()) for slot in range(2)]
    far = [sent(own[slot], even_ahead()) for slot in range(2)]
    passed = [sent(near[slot], even_to_odd()) for slot in range(2)]
    accum = solved(targets, [own[0]], tables)
    accum = solved(targets, [own[1]], tables, accum)
    accum = solved(targets, [near[0]], tables, accum)
    accum = solved(targets, [near[1]], tables, accum)
    accum = solved(targets, [far[0], passed[0]], tables, accum)
    pieces = solved(targets, [far[1], passed[1]], tables, accum, last=True)
    parts = lax.all_to_all(pieces, "col", 0, 0)
    return gathered(parts)


def solution(mesh):
    return jax.shard_map(
        shards,
        mesh=mesh,
        in_specs=(
            P("blk", None, None, None),
            P(("blk", "col"), None, None, None),
            P(("blk", "col")),
            P(),
        ),
        out_specs=P("blk", "col", None, None),
        check_vma=False,
    )
```

```python
import math

import jax
import jax.numpy as jnp
import ml_dtypes
import numpy as np
from jax import lax
from jax.experimental import pallas as pl
from jax.experimental.pallas import tpu as pltpu
from jax.sharding import PartitionSpec as P

NX, NY, NZ = 48, 72, 96
LANES = 128
BASE = 36
TAIL = NX - BASE
HALF_Y = NY // 2 + 1
N_BLK, N_COL = 32, 8
SLICE = NX // N_COL
TILES = SLICE * NY // 8
KEPT = 41
SPARE = TILES - KEPT
AXES = ("blk", "col")
F32, BF16 = jnp.float32, jnp.bfloat16
grid_spacing = 0.3
screening = 0.11


def basis_of(length):
    row, col = np.arange(length)[:, None], np.arange(length)[None, :]
    angle = 2.0 * np.pi / length * (row * col % length)
    table = np.where(row <= length // 2, np.cos(angle), np.sin(angle))
    edge = (row == 0) | (row == length // 2)
    return table * np.where(edge, math.sqrt(1.0 / length), math.sqrt(2.0 / length))


def halves(table):
    high = table.astype(ml_dtypes.bfloat16)
    return high, (table - high.astype(np.float64)).astype(ml_dtypes.bfloat16)


def left_operand(table, pad):
    high, low = halves(table)
    gap = np.zeros((table.shape[0], pad), ml_dtypes.bfloat16)
    return np.concatenate([high, gap, high, gap, low, gap], axis=1)


def right_operand(table):
    size = table.shape[0]
    high, low = halves(table)
    out = np.zeros((2 * LANES, 2 * LANES), ml_dtypes.bfloat16)
    for row in (0, LANES):
        out[row : row + size, :size] = high
        out[row : row + size, LANES : LANES + size] = low
    return out


def frequency_sq(length):
    index = np.arange(length)
    return (2.0 * np.pi * np.minimum(index, length - index) / (length * grid_spacing)) ** 2


def kernel_field():
    g_sq = (
        frequency_sq(NY)[: HALF_Y, None, None]
        + frequency_sq(NX)[None, :, None]
        + frequency_sq(NZ)[None, None, :]
    )
    safe_sq = np.where(g_sq > 0, g_sq, 1.0)
    value = 4.0 * np.pi / safe_sq * (1.0 - np.exp(-safe_sq / (4.0 * screening * screening)))
    value = -0.125 * np.where(g_sq > 0, value, np.pi / (screening * screening))
    out = np.zeros((HALF_Y, NX, LANES), np.float32)
    out[:, :, :NZ] = value
    return out.reshape(HALF_Y * NX, LANES)


def constants():
    basis_x, basis_y, basis_z = basis_of(NX), basis_of(NY), basis_of(NZ)
    tables = (
        kernel_field(),
        left_operand(basis_y, 8),
        left_operand(basis_x, 0),
        right_operand(basis_z.T),
        right_operand(basis_z),
        left_operand(basis_x.T, 0),
        left_operand(basis_y.T, 8),
    )
    return tuple(jnp.asarray(table) for table in tables)


def dot(left, right):
    return jnp.dot(left, right, preferred_element_type=F32)


def split(value):
    high = value.astype(BF16)
    return high, (value - high.astype(F32)).astype(BF16)


def stacked(value):
    high, low = split(value)
    return jnp.concatenate([high, low, high], axis=0)


def stacked_y(value):
    return stacked(jnp.concatenate([value, jnp.zeros((8, LANES), F32)], axis=0))


def side(value):
    high, low = split(value)
    return jnp.concatenate([high, low], axis=1)


def folded(value):
    return value[:, :LANES] + value[:, LANES:]


def columns(value, which):
    return value[:, LANES * which : LANES * (which + 1)]


def widened(value):
    gap = jnp.zeros((value.shape[0], LANES - NZ), F32)
    return jnp.concatenate([value.astype(F32), gap], axis=1)


def lane_of(rows):
    return lax.broadcasted_iota(jnp.int32, (rows, LANES), 1)


def in_hbm(value):
    return pltpu.with_memory_space_constraint(value, pltpu.HBM)


def pack_kernel(band_ref, occupied_ref, source_ref, first_ref, second_ref, held, in_sems):
    chunks = NX // TAIL
    planes = [pl.ds(chunk * TAIL, TAIL) for chunk in range(chunks)]
    order = [(slot, chunk) for slot in range(2) for chunk in (chunks - 1, *range(chunks - 1))]
    reads = {}
    for slot, chunk in order:
        reads[slot, chunk] = pltpu.make_async_copy(
            source_ref.at[slot, planes[chunk]], held.at[slot, planes[chunk]], in_sems.at[slot, chunk]
        )
        reads[slot, chunk].start()
    lane = lane_of(NY)
    for slot, out_ref in enumerate((first_ref, second_ref)):
        weight = jnp.where(occupied_ref[band_ref[slot]] > 0, 1.0, 0.0).astype(F32)
        reads[slot, chunks - 1].wait()
        for third in range(chunks - 1):
            reads[slot, third].wait()
            for index in range(TAIL):
                plane = third * TAIL + index
                base = widened(held[slot, plane])
                tail = pltpu.roll(widened(held[slot, BASE + index]), 96 - 32 * third, 1)
                out_ref[plane] = (jnp.where(lane < 96, base, tail) * weight).astype(BF16)


def packed(sources, band_of_slot, occupied):
    anywhere = pl.BlockSpec(memory_space=pl.ANY)
    whole = pl.BlockSpec(memory_space=pltpu.VMEM)
    scalars = pl.BlockSpec(memory_space=pltpu.SMEM)
    shape = jax.ShapeDtypeStruct((BASE, NY, LANES), BF16)
    return pl.pallas_call(
        pack_kernel,
        out_shape=(shape, shape),
        in_specs=[scalars, scalars, anywhere],
        out_specs=(whole, whole),
        scratch_shapes=[
            pltpu.VMEM((2, NX, NY, NZ), BF16),
            pltpu.SemaphoreType.DMA((2, NX // TAIL)),
        ],
        compiler_params=pltpu.CompilerParams(vmem_limit_bytes=16 << 20),
        name="pack",
    )(*(in_hbm(value) for value in (band_of_slot, occupied, sources)))


def store_piece(accum, out_ref, piece):
    lane = lane_of(8)

    def tile_of(tile):
        plane, row = divmod(tile, NY // 8)
        return accum[piece * SLICE + plane, 8 * row : 8 * row + 8, :]

    largest = jnp.abs(tile_of(0))
    for tile in range(1, TILES):
        largest = jnp.maximum(largest, jnp.abs(tile_of(tile)))
    largest = jnp.max(largest, axis=(0, 1), keepdims=True)
    shift = jnp.floor(jnp.log2(jnp.maximum(largest, 1e-30))) - 14.0
    factor = jnp.broadcast_to(jnp.exp2(-shift), (8, LANES))
    spare = [tile_of(KEPT + index) * factor for index in range(SPARE)]
    for tile in range(KEPT):
        value = tile_of(tile) * factor
        third, index = divmod(tile, SPARE)
        if third < 3:
            value = jnp.where(lane < 96, value, pltpu.roll(spare[index], 96 - 32 * third, 1))
        out_ref[piece, 8 * tile : 8 * tile + 8, :] = value
    out_ref[piece, 8 * KEPT :, :] = jnp.broadcast_to(shift, (8, LANES))


def solve_kernel(*refs, n_sources, has_accum, last):
    target_ref = refs[0]
    source_refs = refs[1 : 1 + n_sources]
    coulomb, left_y, left_x, right_z, right_k, left_p, left_q = refs[1 + n_sources : 8 + n_sources]
    rest = refs[8 + n_sources :]
    if has_accum:
        accum_in, rest = rest[0], rest[1:]
    if not has_accum:
        wide_ref, held_coulomb, *others = rest[1:]
        rest = (rest[0], *others)
    out_ref, by_x, by_y, tail_ref, *more = rest
    if not has_accum:
        fetch = pltpu.make_async_copy(coulomb, held_coulomb, more[0])
        fetch.start()
        coulomb = held_coulomb
    accum = more[0] if last else out_ref

    lane = lane_of(NY)

    def held_plane(plane):
        return sum(ref[plane].astype(F32) for ref in source_refs)

    def first_plane(plane):
        if plane < BASE:
            return held_plane(plane)
        parts = [
            pltpu.roll(held_plane(plane - BASE + third * TAIL), 32 * third + 32, 1) for third in range(3)
        ]
        value = jnp.where(lane < 32, parts[0], jnp.where(lane < 64, parts[1], parts[2]))
        tail_ref[plane - BASE] = value.astype(BF16)
        return value

    def plane_of(plane):
        return held_plane(plane) if plane < BASE else tail_ref[plane - BASE].astype(F32)

    def target_plane(plane):
        if has_accum:
            return target_ref[plane].astype(F32)
        value = widened(target_ref[0, plane])
        wide_ref[plane] = value.astype(BF16)
        return value

    for plane in range(0, NX, 2):
        pair = [target_plane(p) * first_plane(p) for p in (plane, plane + 1)]
        spectrum = dot(left_y[...], jnp.concatenate([stacked_y(p) for p in pair], axis=1))
        for which in range(2):
            by_x[(plane + which) * NY : (plane + which + 1) * NY, :] = columns(spectrum, which)

    if not has_accum:
        fetch.wait()
    group = NY if has_accum else NY // 2

    def middle(step, carry):
        first = step * group
        rows = []
        for row in range(0, group, 2):
            lines = [
                by_x[pl.ds(first + row + which, NX, stride=NY), :] for which in range(2)
            ]
            spectrum = dot(left_x[...], jnp.concatenate([stacked(line) for line in lines], axis=1))
            rows += [side(columns(spectrum, which)) for which in range(2)]
        spectrum = folded(dot(jnp.concatenate(rows, axis=0), right_z[...]))
        field = []
        for row in range(group):
            freq = jnp.minimum(first + row, NY - first - row)
            field.append(coulomb[pl.ds(pl.multiple_of(freq * NX, 8), NX), :])
        spectrum = spectrum * jnp.concatenate(field, axis=0)
        field = folded(dot(side(spectrum), right_k[...]))
        for row in range(0, group, 2):
            lines = [field[(row + which) * NX : (row + which + 1) * NX] for which in range(2)]
            part = dot(left_p[...], jnp.concatenate([stacked(line) for line in lines], axis=1))
            for which in range(2):
                by_y[pl.ds(first + row + which, NX, stride=NY), :] = columns(part, which)
        return carry

    lax.fori_loop(0, NY // group, middle, 0)

    for plane in range(0, NX, 2):
        lines = [by_y[(plane + which) * NY : (plane + which + 1) * NY, :] for which in range(2)]
        potential = dot(left_q[...], jnp.concatenate([stacked_y(line) for line in lines], axis=1))
        for which in range(2):
            term = columns(potential, which) * plane_of(plane + which)
            if has_accum:
                term = term + accum_in[plane + which]
            accum[plane + which] = term
        if last and (plane + 2) % SLICE == 0:
            store_piece(accum, out_ref, plane // SLICE)


def solved(target, source_list, tables, accum=None, last=False):
    whole = pl.BlockSpec(memory_space=pltpu.VMEM)
    operands = [target, *source_list, *tables] + ([accum] if accum is not None else [])
    scratch = [
        pltpu.VMEM((NX * NY, LANES), F32),
        pltpu.VMEM((NX * NY, LANES), F32),
        pltpu.VMEM((TAIL, NY, LANES), BF16),
    ]
    if last:
        shape = (N_COL, 8 * KEPT + 8, LANES)
        scratch.append(pltpu.VMEM((NX, NY, LANES), F32))
    else:
        shape = (NX, NY, LANES)
    out_shape = [jax.ShapeDtypeStruct(shape, F32)]
    if accum is None:
        out_shape.append(jax.ShapeDtypeStruct((NX, NY, LANES), BF16))
        out_shape.append(jax.ShapeDtypeStruct((HALF_Y * NX, LANES), F32))
        scratch.append(pltpu.SemaphoreType.DMA)
    return pl.pallas_call(
        lambda *refs: solve_kernel(
            *refs, n_sources=len(source_list), has_accum=accum is not None, last=last
        ),
        out_shape=out_shape,
        in_specs=[
            pl.BlockSpec(memory_space=pl.ANY) if accum is None and index == 2 else whole
            for index in range(len(operands))
        ],
        out_specs=[whole] * len(out_shape),
        scratch_shapes=scratch,
        compiler_params=pltpu.CompilerParams(vmem_limit_bytes=40 << 20),
        cost_estimate=pl.CostEstimate(flops=2_000_000_000, bytes_accessed=4_000_000, transcendentals=0),
        name="solve",
    )(*operands)


def gather_kernel(total_ref, out_ref):
    lane = lane_of(8)

    def put(tile, value):
        plane, row = divmod(tile, NY // 8)
        out_ref[0, plane, 8 * row : 8 * row + 8, :] = value[:, :NZ]

    for tile in range(KEPT):
        put(tile, total_ref[8 * tile : 8 * tile + 8, :])
    for index in range(SPARE):
        parts = []
        for third in range(3):
            tile = index + third * SPARE
            parts.append(pltpu.roll(total_ref[8 * tile : 8 * tile + 8, :], 32 * third + 32, 1))
        put(KEPT + index, jnp.where(lane < 32, parts[0], jnp.where(lane < 64, parts[1], parts[2])))


def gathered(parts):
    whole = pl.BlockSpec(memory_space=pltpu.VMEM)
    wide = parts.astype(F32)
    total = jnp.sum(wide[:, : 8 * KEPT] * jnp.exp2(wide[:, 8 * KEPT : 8 * KEPT + 1, :1]), axis=0)
    return pl.pallas_call(
        gather_kernel,
        out_shape=jax.ShapeDtypeStruct((1, SLICE, NY, NZ), F32),
        in_specs=[whole],
        out_specs=whole,
        compiler_params=pltpu.CompilerParams(vmem_limit_bytes=16 << 20),
        name="gather",
    )(total)


def flat(block, col):
    return block % N_BLK * N_COL + col


def next_block():
    pairs = []
    for block in range(N_BLK):
        for col in range(N_COL):
            pairs.append((flat(block, col), flat(block + 1, col ^ (block % 2))))
    return pairs


def even_ahead():
    return [(flat(b, c), flat(b + 2, c ^ 1)) for b in range(0, N_BLK, 2) for c in range(N_COL)]


def even_to_odd():
    return [(flat(b, c), flat(b + 1, c)) for b in range(0, N_BLK, 2) for c in range(N_COL)]


def sent(value, pairs):
    return lax.ppermute(value, AXES, pairs)


def shards(targets, sources, band_of_slot, occupied):
    tables = constants()
    own = packed(sources, band_of_slot, occupied)
    near = [sent(own[slot], next_block()) for slot in range(2)]
    far = [sent(own[slot], even_ahead()) for slot in range(2)]
    passed = [sent(near[slot], even_to_odd()) for slot in range(2)]
    accum, target, coulomb = solved(targets, [own[0]], (in_hbm(tables[0]), *tables[1:]))
    tables = (coulomb, *tables[1:])
    (accum,) = solved(target, [own[1]], tables, accum)
    (accum,) = solved(target, [near[0]], tables, accum)
    (accum,) = solved(target, [near[1]], tables, accum)
    (accum,) = solved(target, [far[0], passed[0]], tables, accum)
    (pieces,) = solved(target, [far[1], passed[1]], tables, accum, last=True)
    parts = lax.all_to_all(pieces.astype(jnp.float16), "col", 0, 0)
    return gathered(parts)


def solution(mesh):
    return jax.shard_map(
        shards,
        mesh=mesh,
        in_specs=(
            P("blk", None, None, None),
            P(("blk", "col"), None, None, None),
            P(("blk", "col")),
            P(),
        ),
        out_specs=P("blk", "col", None, None),
        check_vma=False,
    )
```

```python
import math

import jax
import jax.numpy as jnp
import ml_dtypes
import numpy as np
from jax import lax
from jax.experimental import pallas as pl
from jax.experimental.pallas import tpu as pltpu
from jax.sharding import PartitionSpec as P

NX, NY, NZ = 48, 72, 96
LANES = 128
BASE = 36
TAIL = NX - BASE
HALF_Y = NY // 2 + 1
N_BLK, N_COL = 32, 8
SLICE = NX // N_COL
TILES = SLICE * NY // 8
KEPT = 41
SPARE = TILES - KEPT
AXES = ("blk", "col")
F32, BF16 = jnp.float32, jnp.bfloat16
grid_spacing = 0.3
screening = 0.11


def basis_of(length):
    row, col = np.arange(length)[:, None], np.arange(length)[None, :]
    angle = 2.0 * np.pi / length * (row * col % length)
    table = np.where(row <= length // 2, np.cos(angle), np.sin(angle))
    edge = (row == 0) | (row == length // 2)
    return table * np.where(edge, math.sqrt(1.0 / length), math.sqrt(2.0 / length))


def halves(table):
    high = table.astype(ml_dtypes.bfloat16)
    return high, (table - high.astype(np.float64)).astype(ml_dtypes.bfloat16)


def left_operand(table, pad):
    high, low = halves(table)
    gap = np.zeros((table.shape[0], pad), ml_dtypes.bfloat16)
    return np.concatenate([high, gap, high, gap, low, gap], axis=1)


def right_operand(table):
    size = table.shape[0]
    high, low = halves(table)
    out = np.zeros((2 * LANES, 2 * LANES), ml_dtypes.bfloat16)
    for row in (0, LANES):
        out[row : row + size, :size] = high
        out[row : row + size, LANES : LANES + size] = low
    return out


def frequency_sq(length):
    index = np.arange(length)
    return (2.0 * np.pi * np.minimum(index, length - index) / (length * grid_spacing)) ** 2


def kernel_field():
    g_sq = (
        frequency_sq(NY)[: HALF_Y, None, None]
        + frequency_sq(NX)[None, :, None]
        + frequency_sq(NZ)[None, None, :]
    )
    safe_sq = np.where(g_sq > 0, g_sq, 1.0)
    value = 4.0 * np.pi / safe_sq * (1.0 - np.exp(-safe_sq / (4.0 * screening * screening)))
    value = -0.125 * np.where(g_sq > 0, value, np.pi / (screening * screening))
    out = np.zeros((HALF_Y, NX, LANES), np.float32)
    out[:, :, :NZ] = value
    return out.reshape(HALF_Y * NX, LANES)


def constants():
    basis_x, basis_y, basis_z = basis_of(NX), basis_of(NY), basis_of(NZ)
    tables = (
        kernel_field(),
        left_operand(basis_y, 8),
        left_operand(basis_x, 0),
        right_operand(basis_z.T),
        right_operand(basis_z),
        left_operand(basis_x.T, 0),
        left_operand(basis_y.T, 8),
    )
    return tuple(jnp.asarray(table) for table in tables)


def dot(left, right):
    return jnp.dot(left, right, preferred_element_type=F32)


def split(value):
    high = value.astype(BF16)
    return high, (value - high.astype(F32)).astype(BF16)


def stacked(value):
    high, low = split(value)
    return jnp.concatenate([high, low, high], axis=0)


def stacked_y(value):
    return stacked(jnp.concatenate([value, jnp.zeros((8, LANES), F32)], axis=0))


def side(value):
    high, low = split(value)
    return jnp.concatenate([high, low], axis=1)


def folded(value):
    return value[:, :LANES] + value[:, LANES:]


def columns(value, which):
    return value[:, LANES * which : LANES * (which + 1)]


def widened(value):
    gap = jnp.zeros((value.shape[0], LANES - NZ), F32)
    return jnp.concatenate([value.astype(F32), gap], axis=1)


def lane_of(rows):
    return lax.broadcasted_iota(jnp.int32, (rows, LANES), 1)


def in_hbm(value):
    return pltpu.with_memory_space_constraint(value, pltpu.HBM)


def pack_kernel(band_hbm, occupied_hbm, source_ref, out_ref, held, sems, band_ref, occupied_ref, *, slot):
    chunks = NX // TAIL
    lookups = [
        pltpu.make_async_copy(band_hbm, band_ref, sems.at[chunks]),
        pltpu.make_async_copy(occupied_hbm, occupied_ref, sems.at[chunks + 1]),
    ]
    for lookup in lookups:
        lookup.start()
    reads = {}
    for chunk in (chunks - 1, *range(chunks - 1)):
        planes = pl.ds(chunk * TAIL, TAIL)
        reads[chunk] = pltpu.make_async_copy(source_ref.at[slot, planes], held.at[planes], sems.at[chunk])
        reads[chunk].start()
    for lookup in lookups:
        lookup.wait()
    lane = lane_of(NY)
    weight = jnp.where(occupied_ref[band_ref[slot]] > 0, 1.0, 0.0).astype(F32)
    reads[chunks - 1].wait()
    for third in range(chunks - 1):
        reads[third].wait()
        for index in range(TAIL):
            plane = third * TAIL + index
            base = widened(held[plane])
            tail = pltpu.roll(widened(held[BASE + index]), 96 - 32 * third, 1)
            out_ref[plane] = (jnp.where(lane < 96, base, tail) * weight).astype(BF16)


def packed(sources, slot, band_of_slot, occupied):
    anywhere = pl.BlockSpec(memory_space=pl.ANY)
    return pl.pallas_call(
        lambda *refs: pack_kernel(*refs, slot=slot),
        out_shape=jax.ShapeDtypeStruct((BASE, NY, LANES), BF16),
        in_specs=[anywhere] * 3,
        out_specs=pl.BlockSpec(memory_space=pltpu.VMEM),
        scratch_shapes=[
            pltpu.VMEM((NX, NY, NZ), BF16),
            pltpu.SemaphoreType.DMA((NX // TAIL + 2,)),
            pltpu.SMEM(band_of_slot.shape, jnp.int32),
            pltpu.SMEM(occupied.shape, jnp.int32),
        ],
        compiler_params=pltpu.CompilerParams(vmem_limit_bytes=16 << 20),
        name="pack",
    )(*(in_hbm(value) for value in (band_of_slot, occupied, sources)))


def store_piece(accum, out_ref, piece):
    lane = lane_of(8)

    def tile_of(tile):
        plane, row = divmod(tile, NY // 8)
        return accum[piece * SLICE + plane, 8 * row : 8 * row + 8, :]

    largest = jnp.abs(tile_of(0))
    for tile in range(1, TILES):
        largest = jnp.maximum(largest, jnp.abs(tile_of(tile)))
    largest = jnp.max(largest, axis=(0, 1), keepdims=True)
    shift = jnp.floor(jnp.log2(jnp.maximum(largest, 1e-30))) - 14.0
    factor = jnp.broadcast_to(jnp.exp2(-shift), (8, LANES))
    spare = [tile_of(KEPT + index) * factor for index in range(SPARE)]
    for tile in range(KEPT):
        value = tile_of(tile) * factor
        third, index = divmod(tile, SPARE)
        if third < 3:
            value = jnp.where(lane < 96, value, pltpu.roll(spare[index], 96 - 32 * third, 1))
        out_ref[piece, 8 * tile : 8 * tile + 8, :] = value
    out_ref[piece, 8 * KEPT :, :] = jnp.broadcast_to(shift, (8, LANES))


def solve_kernel(*refs, n_sources, has_accum, last):
    target_ref = refs[0]
    source_refs = refs[1 : 1 + n_sources]
    coulomb, left_y, left_x, right_z, right_k, left_p, left_q = refs[1 + n_sources : 8 + n_sources]
    rest = refs[8 + n_sources :]
    if has_accum:
        accum_in, rest = rest[0], rest[1:]
    if not has_accum:
        wide_ref, held_coulomb, *others = rest[1:]
        rest = (rest[0], *others)
    out_ref, by_x, by_y, tail_ref, *more = rest
    if not has_accum:
        fetch = pltpu.make_async_copy(coulomb, held_coulomb, more[0])
        fetch.start()
        coulomb = held_coulomb
    accum = more[0] if last else out_ref

    lane = lane_of(NY)

    def held_plane(plane):
        return sum(ref[plane].astype(F32) for ref in source_refs)

    def first_plane(plane):
        if plane < BASE:
            return held_plane(plane)
        parts = [
            pltpu.roll(held_plane(plane - BASE + third * TAIL), 32 * third + 32, 1) for third in range(3)
        ]
        value = jnp.where(lane < 32, parts[0], jnp.where(lane < 64, parts[1], parts[2]))
        tail_ref[plane - BASE] = value.astype(BF16)
        return value

    def plane_of(plane):
        return held_plane(plane) if plane < BASE else tail_ref[plane - BASE].astype(F32)

    def target_plane(plane):
        if has_accum:
            return target_ref[plane].astype(F32)
        value = widened(target_ref[0, plane])
        wide_ref[plane] = value.astype(BF16)
        return value

    for plane in range(0, NX, 2):
        pair = [target_plane(p) * first_plane(p) for p in (plane, plane + 1)]
        spectrum = dot(left_y[...], jnp.concatenate([stacked_y(p) for p in pair], axis=1))
        for which in range(2):
            by_x[(plane + which) * NY : (plane + which + 1) * NY, :] = columns(spectrum, which)

    if not has_accum:
        fetch.wait()
    group = NY if has_accum else NY // 2

    def middle(step, carry):
        first = step * group
        rows = []
        for row in range(0, group, 2):
            lines = [
                by_x[pl.ds(first + row + which, NX, stride=NY), :] for which in range(2)
            ]
            spectrum = dot(left_x[...], jnp.concatenate([stacked(line) for line in lines], axis=1))
            rows += [side(columns(spectrum, which)) for which in range(2)]
        spectrum = folded(dot(jnp.concatenate(rows, axis=0), right_z[...]))
        field = []
        for row in range(group):
            freq = jnp.minimum(first + row, NY - first - row)
            field.append(coulomb[pl.ds(pl.multiple_of(freq * NX, 8), NX), :])
        spectrum = spectrum * jnp.concatenate(field, axis=0)
        field = folded(dot(side(spectrum), right_k[...]))
        for row in range(0, group, 2):
            lines = [field[(row + which) * NX : (row + which + 1) * NX] for which in range(2)]
            part = dot(left_p[...], jnp.concatenate([stacked(line) for line in lines], axis=1))
            for which in range(2):
                by_y[pl.ds(first + row + which, NX, stride=NY), :] = columns(part, which)
        return carry

    lax.fori_loop(0, NY // group, middle, 0)

    for plane in range(0, NX, 2):
        lines = [by_y[(plane + which) * NY : (plane + which + 1) * NY, :] for which in range(2)]
        potential = dot(left_q[...], jnp.concatenate([stacked_y(line) for line in lines], axis=1))
        for which in range(2):
            term = columns(potential, which) * plane_of(plane + which)
            if has_accum:
                term = term + accum_in[plane + which]
            accum[plane + which] = term
        if last and (plane + 2) % SLICE == 0:
            store_piece(accum, out_ref, plane // SLICE)


def solved(target, source_list, tables, accum=None, last=False):
    whole = pl.BlockSpec(memory_space=pltpu.VMEM)
    operands = [target, *source_list, *tables] + ([accum] if accum is not None else [])
    scratch = [
        pltpu.VMEM((NX * NY, LANES), F32),
        pltpu.VMEM((NX * NY, LANES), F32),
        pltpu.VMEM((TAIL, NY, LANES), BF16),
    ]
    if last:
        shape = (N_COL, 8 * KEPT + 8, LANES)
        scratch.append(pltpu.VMEM((NX, NY, LANES), F32))
    else:
        shape = (NX, NY, LANES)
    out_shape = [jax.ShapeDtypeStruct(shape, F32)]
    if accum is None:
        out_shape.append(jax.ShapeDtypeStruct((NX, NY, LANES), BF16))
        out_shape.append(jax.ShapeDtypeStruct((HALF_Y * NX, LANES), F32))
        scratch.append(pltpu.SemaphoreType.DMA)
    return pl.pallas_call(
        lambda *refs: solve_kernel(
            *refs, n_sources=len(source_list), has_accum=accum is not None, last=last
        ),
        out_shape=out_shape,
        in_specs=[
            pl.BlockSpec(memory_space=pl.ANY) if accum is None and index == 2 else whole
            for index in range(len(operands))
        ],
        out_specs=[whole] * len(out_shape),
        scratch_shapes=scratch,
        compiler_params=pltpu.CompilerParams(vmem_limit_bytes=40 << 20),
        cost_estimate=pl.CostEstimate(flops=2_000_000_000, bytes_accessed=4_000_000, transcendentals=0),
        name="solve",
    )(*operands)


def gather_kernel(total_ref, out_ref):
    lane = lane_of(8)

    def put(tile, value):
        plane, row = divmod(tile, NY // 8)
        out_ref[0, plane, 8 * row : 8 * row + 8, :] = value[:, :NZ]

    for tile in range(KEPT):
        put(tile, total_ref[8 * tile : 8 * tile + 8, :])
    for index in range(SPARE):
        parts = []
        for third in range(3):
            tile = index + third * SPARE
            parts.append(pltpu.roll(total_ref[8 * tile : 8 * tile + 8, :], 32 * third + 32, 1))
        put(KEPT + index, jnp.where(lane < 32, parts[0], jnp.where(lane < 64, parts[1], parts[2])))


def gathered(parts):
    whole = pl.BlockSpec(memory_space=pltpu.VMEM)
    wide = parts.astype(F32)
    total = jnp.sum(wide[:, : 8 * KEPT] * jnp.exp2(wide[:, 8 * KEPT : 8 * KEPT + 1, :1]), axis=0)
    return pl.pallas_call(
        gather_kernel,
        out_shape=jax.ShapeDtypeStruct((1, SLICE, NY, NZ), F32),
        in_specs=[whole],
        out_specs=whole,
        compiler_params=pltpu.CompilerParams(vmem_limit_bytes=16 << 20),
        name="gather",
    )(total)


def flat(block, col):
    return block % N_BLK * N_COL + col


def next_block():
    pairs = []
    for block in range(N_BLK):
        for col in range(N_COL):
            pairs.append((flat(block, col), flat(block + 1, col ^ (block % 2))))
    return pairs


def even_ahead():
    return [(flat(b, c), flat(b + 2, c ^ 1)) for b in range(0, N_BLK, 2) for c in range(N_COL)]


def even_to_odd():
    return [(flat(b, c), flat(b + 1, c)) for b in range(0, N_BLK, 2) for c in range(N_COL)]


def sent(value, pairs):
    return lax.ppermute(value, AXES, pairs)


def shards(targets, sources, band_of_slot, occupied):
    tables = constants()
    own = []
    for slot in range(2):
        own.append(packed(sources, slot, band_of_slot, occupied))
    near = [sent(own[slot], next_block()) for slot in range(2)]
    far = [sent(own[slot], even_ahead()) for slot in range(2)]
    passed = [sent(near[slot], even_to_odd()) for slot in range(2)]
    accum, target, coulomb = solved(targets, [own[0]], (in_hbm(tables[0]), *tables[1:]))
    tables = (coulomb, *tables[1:])
    (accum,) = solved(target, [own[1]], tables, accum)
    (accum,) = solved(target, [near[0]], tables, accum)
    (accum,) = solved(target, [near[1]], tables, accum)
    (accum,) = solved(target, [far[0], passed[0]], tables, accum)
    (pieces,) = solved(target, [far[1], passed[1]], tables, accum, last=True)
    parts = lax.all_to_all(pieces.astype(jnp.float16), "col", 0, 0)
    return gathered(parts)


def solution(mesh):
    return jax.shard_map(
        shards,
        mesh=mesh,
        in_specs=(
            P("blk", None, None, None),
            P(("blk", "col"), None, None, None),
            P(("blk", "col")),
            P(),
        ),
        out_specs=P("blk", "col", None, None),
        check_vma=False,
    )
```

```python
import math

import jax
import jax.numpy as jnp
import ml_dtypes
import numpy as np
from jax import lax
from jax.experimental import pallas as pl
from jax.experimental.pallas import tpu as pltpu
from jax.sharding import PartitionSpec as P

NX, NY, NZ = 48, 72, 96
LANES = 128
BASE = 36
TAIL = NX - BASE
HALF_Y = NY // 2 + 1
N_BLK, N_COL = 32, 8
SLICE = NX // N_COL
TILES = SLICE * NY // 8
KEPT = 41
SPARE = TILES - KEPT
AXES = ("blk", "col")
F32, BF16 = jnp.float32, jnp.bfloat16
grid_spacing = 0.3
screening = 0.11


def basis_of(length):
    row, col = np.arange(length)[:, None], np.arange(length)[None, :]
    angle = 2.0 * np.pi / length * (row * col % length)
    table = np.where(row <= length // 2, np.cos(angle), np.sin(angle))
    edge = (row == 0) | (row == length // 2)
    return table * np.where(edge, math.sqrt(1.0 / length), math.sqrt(2.0 / length))


def halves(table):
    high = table.astype(ml_dtypes.bfloat16)
    return high, (table - high.astype(np.float64)).astype(ml_dtypes.bfloat16)


def left_operand(table, pad):
    high, low = halves(table)
    gap = np.zeros((table.shape[0], pad), ml_dtypes.bfloat16)
    return np.concatenate([high, gap, high, gap, low, gap], axis=1)


def right_operand(table):
    size = table.shape[0]
    high, low = halves(table)
    out = np.zeros((2 * LANES, 2 * LANES), ml_dtypes.bfloat16)
    for row in (0, LANES):
        out[row : row + size, :size] = high
        out[row : row + size, LANES : LANES + size] = low
    return out


def frequency_sq(length):
    index = np.arange(length)
    return (2.0 * np.pi * np.minimum(index, length - index) / (length * grid_spacing)) ** 2


def kernel_field():
    g_sq = (
        frequency_sq(NY)[: HALF_Y, None, None]
        + frequency_sq(NX)[None, :, None]
        + frequency_sq(NZ)[None, None, :]
    )
    safe_sq = np.where(g_sq > 0, g_sq, 1.0)
    value = 4.0 * np.pi / safe_sq * (1.0 - np.exp(-safe_sq / (4.0 * screening * screening)))
    value = -0.125 * np.where(g_sq > 0, value, np.pi / (screening * screening))
    out = np.zeros((HALF_Y, NX, LANES), np.float32)
    out[:, :, :NZ] = value
    return out.reshape(HALF_Y * NX, LANES)


def constants():
    basis_x, basis_y, basis_z = basis_of(NX), basis_of(NY), basis_of(NZ)
    tables = (
        kernel_field(),
        left_operand(basis_y, 8),
        left_operand(basis_x, 0),
        right_operand(basis_z.T),
        right_operand(basis_z),
        left_operand(basis_x.T, 0),
        left_operand(basis_y.T, 8),
    )
    return tuple(jnp.asarray(table) for table in tables)


def dot(left, right):
    return jnp.dot(left, right, preferred_element_type=F32)


def split(value):
    high = value.astype(BF16)
    return high, (value - high.astype(F32)).astype(BF16)


def stacked(value):
    high, low = split(value)
    return jnp.concatenate([high, low, high], axis=0)


def stacked_y(value):
    return stacked(jnp.concatenate([value, jnp.zeros((8, LANES), F32)], axis=0))


def side(value):
    high, low = split(value)
    return jnp.concatenate([high, low], axis=1)


def folded(value):
    return value[:, :LANES] + value[:, LANES:]


def columns(value, which):
    return value[:, LANES * which : LANES * (which + 1)]


def widened(value):
    gap = jnp.zeros((value.shape[0], LANES - NZ), F32)
    return jnp.concatenate([value.astype(F32), gap], axis=1)


def lane_of(rows):
    return lax.broadcasted_iota(jnp.int32, (rows, LANES), 1)


def in_hbm(value):
    return pltpu.with_memory_space_constraint(value, pltpu.HBM)


def pack_kernel(band_hbm, occupied_hbm, source_ref, out_ref, held, sems, band_ref, occupied_ref, *, slot):
    chunks = NX // TAIL
    lookups = [
        pltpu.make_async_copy(band_hbm, band_ref, sems.at[chunks]),
        pltpu.make_async_copy(occupied_hbm, occupied_ref, sems.at[chunks + 1]),
    ]
    for lookup in lookups:
        lookup.start()
    reads = {}
    for chunk in (chunks - 1, *range(chunks - 1)):
        planes = pl.ds(chunk * TAIL, TAIL)
        reads[chunk] = pltpu.make_async_copy(source_ref.at[slot, planes], held.at[planes], sems.at[chunk])
        reads[chunk].start()
    for lookup in lookups:
        lookup.wait()
    lane = lane_of(NY)
    weight = jnp.where(occupied_ref[band_ref[slot]] > 0, 1.0, 0.0).astype(F32)
    reads[chunks - 1].wait()
    for third in range(chunks - 1):
        reads[third].wait()
        for index in range(TAIL):
            plane = third * TAIL + index
            base = widened(held[plane])
            tail = pltpu.roll(widened(held[BASE + index]), 96 - 32 * third, 1)
            out_ref[plane] = (jnp.where(lane < 96, base, tail) * weight).astype(BF16)


def packed(sources, slot, band_of_slot, occupied):
    anywhere = pl.BlockSpec(memory_space=pl.ANY)
    return pl.pallas_call(
        lambda *refs: pack_kernel(*refs, slot=slot),
        out_shape=jax.ShapeDtypeStruct((BASE, NY, LANES), BF16),
        in_specs=[anywhere] * 3,
        out_specs=pl.BlockSpec(memory_space=pltpu.VMEM),
        scratch_shapes=[
            pltpu.VMEM((NX, NY, NZ), BF16),
            pltpu.SemaphoreType.DMA((NX // TAIL + 2,)),
            pltpu.SMEM(band_of_slot.shape, jnp.int32),
            pltpu.SMEM(occupied.shape, jnp.int32),
        ],
        compiler_params=pltpu.CompilerParams(vmem_limit_bytes=16 << 20),
        name="pack",
    )(*(in_hbm(value) for value in (band_of_slot, occupied, sources)))


def store_piece(accum, out_ref, piece):
    lane = lane_of(8)

    def tile_of(tile):
        plane, row = divmod(tile, NY // 8)
        return accum[piece * SLICE + plane, 8 * row : 8 * row + 8, :]

    largest = jnp.abs(tile_of(0))
    for tile in range(1, TILES):
        largest = jnp.maximum(largest, jnp.abs(tile_of(tile)))
    largest = jnp.max(largest, axis=(0, 1), keepdims=True)
    shift = jnp.floor(jnp.log2(jnp.maximum(largest, 1e-30))) - 14.0
    factor = jnp.broadcast_to(jnp.exp2(-shift), (8, LANES))
    spare = [tile_of(KEPT + index) * factor for index in range(SPARE)]
    for tile in range(KEPT):
        value = tile_of(tile) * factor
        third, index = divmod(tile, SPARE)
        if third < 3:
            value = jnp.where(lane < 96, value, pltpu.roll(spare[index], 96 - 32 * third, 1))
        out_ref[piece, 8 * tile : 8 * tile + 8, :] = value
    out_ref[piece, 8 * KEPT :, :] = jnp.broadcast_to(shift, (8, LANES))


def solve_kernel(*refs, n_sources, has_accum, last):
    target_ref = refs[0]
    source_refs = refs[1 : 1 + n_sources]
    coulomb, left_y, left_x, right_z, right_k, left_p, left_q = refs[1 + n_sources : 8 + n_sources]
    rest = refs[8 + n_sources :]
    if has_accum:
        accum_in, rest = rest[0], rest[1:]
    if not has_accum:
        wide_ref, held_coulomb, *others = rest[1:]
        rest = (rest[0], *others)
    out_ref, by_x, by_y, tail_ref, *more = rest
    if not has_accum:
        fetch = pltpu.make_async_copy(coulomb, held_coulomb, more[0])
        fetch.start()
        coulomb = held_coulomb
    accum = more[0] if last else out_ref

    lane = lane_of(NY)

    def held_plane(plane):
        value = source_refs[0][plane]
        for ref in source_refs[1:]:
            value = value + ref[plane]
        return value.astype(F32)

    def first_plane(plane):
        if plane < BASE:
            return held_plane(plane)
        parts = [
            pltpu.roll(held_plane(plane - BASE + third * TAIL), 32 * third + 32, 1) for third in range(3)
        ]
        value = jnp.where(lane < 32, parts[0], jnp.where(lane < 64, parts[1], parts[2]))
        tail_ref[plane - BASE] = value.astype(BF16)
        return value

    def plane_of(plane):
        return held_plane(plane) if plane < BASE else tail_ref[plane - BASE].astype(F32)

    def target_plane(plane):
        if has_accum:
            return target_ref[plane].astype(F32)
        value = widened(target_ref[0, plane])
        wide_ref[plane] = value.astype(BF16)
        return value

    for plane in range(0, NX, 2):
        pair = [target_plane(p) * first_plane(p) for p in (plane, plane + 1)]
        spectrum = dot(left_y[...], jnp.concatenate([stacked_y(p) for p in pair], axis=1))
        for which in range(2):
            by_x[(plane + which) * NY : (plane + which + 1) * NY, :] = columns(spectrum, which)

    if not has_accum:
        fetch.wait()
    group = NY if has_accum else NY // 2

    def middle(step, carry):
        first = step * group
        rows = []
        for row in range(0, group, 2):
            lines = [
                by_x[pl.ds(first + row + which, NX, stride=NY), :] for which in range(2)
            ]
            spectrum = dot(left_x[...], jnp.concatenate([stacked(line) for line in lines], axis=1))
            rows += [side(columns(spectrum, which)) for which in range(2)]
        spectrum = folded(dot(jnp.concatenate(rows, axis=0), right_z[...]))
        field = []
        for row in range(group):
            freq = jnp.minimum(first + row, NY - first - row)
            field.append(coulomb[pl.ds(pl.multiple_of(freq * NX, 8), NX), :])
        spectrum = spectrum * jnp.concatenate(field, axis=0)
        field = folded(dot(side(spectrum), right_k[...]))
        for row in range(0, group, 2):
            lines = [field[(row + which) * NX : (row + which + 1) * NX] for which in range(2)]
            part = dot(left_p[...], jnp.concatenate([stacked(line) for line in lines], axis=1))
            for which in range(2):
                by_y[pl.ds(first + row + which, NX, stride=NY), :] = columns(part, which)
        return carry

    lax.fori_loop(0, NY // group, middle, 0)

    for plane in range(0, NX, 2):
        lines = [by_y[(plane + which) * NY : (plane + which + 1) * NY, :] for which in range(2)]
        potential = dot(left_q[...], jnp.concatenate([stacked_y(line) for line in lines], axis=1))
        for which in range(2):
            term = columns(potential, which) * plane_of(plane + which)
            if has_accum:
                term = term + accum_in[plane + which]
            accum[plane + which] = term
        if last and (plane + 2) % SLICE == 0:
            store_piece(accum, out_ref, plane // SLICE)


def solved(target, source_list, tables, accum=None, last=False):
    whole = pl.BlockSpec(memory_space=pltpu.VMEM)
    operands = [target, *source_list, *tables] + ([accum] if accum is not None else [])
    scratch = [
        pltpu.VMEM((NX * NY, LANES), F32),
        pltpu.VMEM((NX * NY, LANES), F32),
        pltpu.VMEM((TAIL, NY, LANES), BF16),
    ]
    if last:
        shape = (N_COL, 8 * KEPT + 8, LANES)
        scratch.append(pltpu.VMEM((NX, NY, LANES), F32))
    else:
        shape = (NX, NY, LANES)
    out_shape = [jax.ShapeDtypeStruct(shape, F32)]
    if accum is None:
        out_shape.append(jax.ShapeDtypeStruct((NX, NY, LANES), BF16))
        out_shape.append(jax.ShapeDtypeStruct((HALF_Y * NX, LANES), F32))
        scratch.append(pltpu.SemaphoreType.DMA)
    return pl.pallas_call(
        lambda *refs: solve_kernel(
            *refs, n_sources=len(source_list), has_accum=accum is not None, last=last
        ),
        out_shape=out_shape,
        in_specs=[
            pl.BlockSpec(memory_space=pl.ANY) if accum is None and index == 2 else whole
            for index in range(len(operands))
        ],
        out_specs=[whole] * len(out_shape),
        scratch_shapes=scratch,
        compiler_params=pltpu.CompilerParams(vmem_limit_bytes=40 << 20),
        cost_estimate=pl.CostEstimate(flops=2_000_000_000, bytes_accessed=4_000_000, transcendentals=0),
        name="solve",
    )(*operands)


def gather_kernel(total_ref, out_ref):
    lane = lane_of(8)

    def put(tile, value):
        plane, row = divmod(tile, NY // 8)
        out_ref[0, plane, 8 * row : 8 * row + 8, :] = value[:, :NZ]

    for tile in range(KEPT):
        put(tile, total_ref[8 * tile : 8 * tile + 8, :])
    for index in range(SPARE):
        parts = []
        for third in range(3):
            tile = index + third * SPARE
            parts.append(pltpu.roll(total_ref[8 * tile : 8 * tile + 8, :], 32 * third + 32, 1))
        put(KEPT + index, jnp.where(lane < 32, parts[0], jnp.where(lane < 64, parts[1], parts[2])))


def gathered(parts):
    whole = pl.BlockSpec(memory_space=pltpu.VMEM)
    scale = jnp.exp2(parts[:, 8 * KEPT : 8 * KEPT + 1, :1].astype(F32))
    total = jnp.sum(parts[:, : 8 * KEPT].astype(F32) * scale, axis=0)
    return pl.pallas_call(
        gather_kernel,
        out_shape=jax.ShapeDtypeStruct((1, SLICE, NY, NZ), F32),
        in_specs=[whole],
        out_specs=whole,
        compiler_params=pltpu.CompilerParams(vmem_limit_bytes=16 << 20),
        name="gather",
    )(total)


def flat(block, col):
    return block % N_BLK * N_COL + col


def next_block():
    pairs = []
    for block in range(N_BLK):
        for col in range(N_COL):
            pairs.append((flat(block, col), flat(block + 1, col ^ (block % 2))))
    return pairs


def even_ahead():
    return [(flat(b, c), flat(b + 2, c ^ 1)) for b in range(0, N_BLK, 2) for c in range(N_COL)]


def even_to_odd():
    return [(flat(b, c), flat(b + 1, c)) for b in range(0, N_BLK, 2) for c in range(N_COL)]


def sent(value, pairs):
    return lax.ppermute(value, AXES, pairs)


def shards(targets, sources, band_of_slot, occupied):
    tables = constants()
    own = []
    for slot in range(2):
        own.append(packed(sources, slot, band_of_slot, occupied))
    near = [sent(own[slot], next_block()) for slot in range(2)]
    far = [sent(own[slot], even_ahead()) for slot in range(2)]
    passed = [sent(near[slot], even_to_odd()) for slot in range(2)]
    accum, target, coulomb = solved(targets, [own[0]], (in_hbm(tables[0]), *tables[1:]))
    tables = (coulomb, *tables[1:])
    (accum,) = solved(target, [own[1]], tables, accum)
    (accum,) = solved(target, [near[0]], tables, accum)
    (accum,) = solved(target, [near[1]], tables, accum)
    (accum,) = solved(target, [far[0], passed[0]], tables, accum)
    (pieces,) = solved(target, [far[1], passed[1]], tables, accum, last=True)
    parts = lax.all_to_all(pieces.astype(jnp.float16), "col", 0, 0)
    return gathered(parts)


def solution(mesh):
    return jax.shard_map(
        shards,
        mesh=mesh,
        in_specs=(
            P("blk", None, None, None),
            P(("blk", "col"), None, None, None),
            P(("blk", "col")),
            P(),
        ),
        out_specs=P("blk", "col", None, None),
        check_vma=False,
    )
```
